32 devices in a mesh: prec: 16 (over z, x, core), run: 2 (over y).
Axes of the slice: x: 2, y: 2, z: 4, core: 2. Of those that a mesh axis runs over, the one named last changes fastest.
Arguments:
- intensity: bfloat16 [1024, 32768], P('run', 'prec'), may hold values from -6 to 6
- observed: int32 [1024, 4096], P('run', 'prec'), may hold values from 0 to 255, as said below
- run_factors: bfloat16 [1024, 64], P('run'), as said below
- prec_factors: bfloat16 [32768, 64], P('prec'), as said below
Outputs:
- completed: bfloat16 [1024, 32768], P('run', 'prec')
The draws below stay inside these ranges and needn't reach their ends.
Inputs may be any that keep to these rules, and one draw needn't show every extreme that they name: `observed`: each word packs eight observation flags in its low 8 bits: bit b of word j is the flag of precursor 8 j + b. `run_factors`: rows of the starting factors have scales that vary along the rows. `prec_factors`: rows of the starting factors have scales that vary along the rows.
All inputs are finite; a program needn't handle non-finite values.
Results may differ from the reference program's by a relative error of at most 0.005.
Values may be sent and summed in bfloat16 or wider, within the bound.
A program may use at most 64 MiB of HBM per device.

```python
import jax
import jax.numpy as jnp
from jax import lax

P_SIZE = 32768
K = 64
ITERS = 4
R = 1024


def scaled_rows(key, rows, cols):
    base = jax.random.normal(key, (rows, cols), jnp.float32)
    place = jnp.arange(rows, dtype=jnp.float32) / rows
    scale = 0.25 * jnp.exp(jnp.log(3.0) * place)
    return (base * scale[:, None]).astype(jnp.bfloat16)


def draw_run_factors(key, part):
    return scaled_rows(jax.random.fold_in(key, 11), R, K)


def draw_prec_factors(key, part):
    return scaled_rows(jax.random.fold_in(key, 23), P_SIZE, K)


def draw_observed(key, part):
    base = jax.random.fold_in(key, 37)
    words = P_SIZE // 8
    first = jax.random.randint(jax.random.fold_in(base, 1), (R, words), 0, 256)
    second = jax.random.randint(jax.random.fold_in(base, 2), (R, words), 0, 256)
    third = jax.random.randint(jax.random.fold_in(base, 3), (R, words), 0, 256)
    packed = first | second | third
    window = jax.random.randint(jax.random.fold_in(base, 4), (R // 64, words), 0, 5)
    keep = jnp.repeat((window != 0).astype(jnp.int32), 64, axis=0)
    result = (packed * keep).astype(jnp.int32)
    result = result.at[0, 0].set(255)
    result = result.at[R - 1, words - 1].set(0)
    return result


def block_levels(key, dims, shards, low, top_value):
    def one(position, blocks):
        heights = jax.random.uniform(jax.random.fold_in(jax.random.fold_in(key, 6), position), (blocks,), jnp.float32, low / len(shards), top_value / len(shards))
        return jnp.repeat(jnp.exp(heights), dims[position] // blocks).reshape((-1,) + (1,) * (len(dims) - position - 1))

    factor_of = one(*shards[0])
    for cut in shards[1:]:
        factor_of = factor_of * one(*cut)
    return factor_of


def gaussian(rng, extent, scale, reach, shards=(), kind=jnp.bfloat16):
    factor_of = block_levels(rng, extent, shards, -0.22, 0.18) if shards else 1.0
    drawn = jax.random.normal(rng, extent, jnp.float32) * scale * factor_of
    return jnp.minimum(jnp.maximum(drawn, -reach), reach).astype(kind)


def setup_inputs(seed: int = 0) -> dict:
    splits = jax.random.split(jax.random.key(seed), 5)
    intensity = gaussian(splits[0], (R, P_SIZE), 1.0, 6.0, ((0, 2), (1, 16)))
    observed = draw_observed(jax.random.fold_in(splits[4], 71), 0)
    run_factors = draw_run_factors(jax.random.fold_in(splits[4], 71), 0)
    prec_factors = draw_prec_factors(jax.random.fold_in(splits[4], 71), 0)
    return {"intensity": intensity, "observed": observed, "run_factors": run_factors, "prec_factors": prec_factors}


ridge_value = 16.0
block_rows = 1024

def unpack_mask(words):
    shifts = jnp.arange(8, dtype=jnp.int32)
    bits = jnp.right_shift(words[:, :, None], shifts) & 1
    return bits.reshape(words.shape[0], -1).astype(jnp.float32)

def ridge_solve(matrix, gram):
    size = gram.shape[0]
    factor = jnp.linalg.cholesky(gram + ridge_value * jnp.eye(size, dtype=jnp.float32))
    return jax.scipy.linalg.cho_solve((factor, True), matrix.T).T

def reference(intensity, observed, run_factors, prec_factors):
    rows_all = intensity.shape[0]
    block = min(block_rows, rows_all)
    nblocks = rows_all // block
    inten_blocks = intensity.reshape(nblocks, block, -1)
    mask_blocks = observed.reshape(nblocks, block, -1)
    u_now = run_factors
    v_now = prec_factors
    for step in range(ITERS):
        gram_v = jnp.dot(v_now.T.astype(jnp.float32), v_now.astype(jnp.float32), preferred_element_type=jnp.float32)
        u_blocks = u_now.reshape(nblocks, block, -1)

        def update_u(items):
            inten, words, u_blk = items
            fit = jnp.dot(u_blk.astype(jnp.float32), v_now.T.astype(jnp.float32), preferred_element_type=jnp.float32)
            resid = (unpack_mask(words) * (inten.astype(jnp.float32) - fit)).astype(jnp.bfloat16)
            proj = jnp.dot(resid.astype(jnp.float32), v_now.astype(jnp.float32), preferred_element_type=jnp.float32)
            total = jnp.dot(u_blk.astype(jnp.float32), gram_v, precision=lax.Precision.HIGHEST) + proj
            return ridge_solve(total, gram_v).astype(jnp.bfloat16)
        u_now = lax.map(update_u, (inten_blocks, mask_blocks, u_blocks)).reshape(rows_all, -1)
        gram_u = jnp.dot(u_now.T.astype(jnp.float32), u_now.astype(jnp.float32), preferred_element_type=jnp.float32)
        u_blocks = u_now.reshape(nblocks, block, -1)

        def add_proj(carry, items):
            inten, words, u_blk = items
            fit = jnp.dot(u_blk.astype(jnp.float32), v_now.T.astype(jnp.float32), preferred_element_type=jnp.float32)
            resid = (unpack_mask(words) * (inten.astype(jnp.float32) - fit)).astype(jnp.bfloat16)
            return (carry + jnp.dot(resid.T.astype(jnp.float32), u_blk.astype(jnp.float32), preferred_element_type=jnp.float32), None)
        start = jnp.zeros(v_now.shape, jnp.float32)
        proj_v, unused = lax.scan(add_proj, start, (inten_blocks, mask_blocks, u_blocks))
        total = jnp.dot(v_now.astype(jnp.float32), gram_u, precision=lax.Precision.HIGHEST) + proj_v
        v_now = ridge_solve(total, gram_u).astype(jnp.bfloat16)
    u_blocks = u_now.reshape(nblocks, block, -1)

    def finish(items):
        inten, words, u_blk = items
        fit = jnp.dot(u_blk.astype(jnp.float32), v_now.T.astype(jnp.float32), preferred_element_type=jnp.float32)
        maskf = unpack_mask(words)
        return (maskf * inten.astype(jnp.float32) + (1.0 - maskf) * fit).astype(jnp.bfloat16)
    return lax.map(finish, (inten_blocks, mask_blocks, u_blocks)).reshape(rows_all, -1)
```

```python
import functools

import jax
import jax.numpy as jnp
from jax import lax
from jax.experimental import pallas as pl
from jax.experimental.pallas import tpu as pltpu
from jax.sharding import PartitionSpec as P

ITERS = 4
ridge_value = 16.0
f32 = jnp.float32
bf16 = jnp.bfloat16
MESH = pl.DeviceIdType.MESH


def mm(a, b):
    return lax.dot_general(a, b, (((1,), (0,)), ((), ())), preferred_element_type=f32)


def mm_nt(a, b):
    return lax.dot_general(a, b, (((1,), (1,)), ((), ())), preferred_element_type=f32)


def spd_inverse(a):
    size = a.shape[0]
    wide = 2 * size
    rid = lax.broadcasted_iota(jnp.int32, (size, wide), 0)
    eye = (
        lax.broadcasted_iota(jnp.int32, (size, size), 0)
        == lax.broadcasted_iota(jnp.int32, (size, size), 1)
    ).astype(f32)
    m = jnp.concatenate([a + ridge_value * eye, eye], axis=1)
    group = 4
    for k0 in range(0, size, group):
        cols = [
            jnp.broadcast_to(m[:, k0 + j : k0 + j + 1], (size, wide)) for j in range(group)
        ]
        for j in range(group):
            k = k0 + j
            inv = 1.0 / cols[j][k : k + 1, :]
            prow = m[k : k + 1, :] * inv
            m = jnp.where(rid == k, prow, m - cols[j] * prow)
            for n in range(j + 1, group):
                f = cols[j][k0 + n : k0 + n + 1, :] * inv
                cols[n] = jnp.where(rid == k, f, cols[n] - cols[j] * f)
    return m[:, size:]


def split(x):
    hi = x.astype(bf16)
    return hi, (x - hi.astype(f32)).astype(bf16)


def pack_gram(g):
    h = g.shape[0] // 2
    return jnp.concatenate([g[:h], g[h:]], axis=1)


def unpack_gram(x):
    h = x.shape[1] // 2
    return jnp.concatenate([x[:, :h], x[:, h:]], axis=0)


def als_kernel(
    n, nr, fold, uchunks, vchunks,
    x_ref, w_ref, u0_ref, v0_ref, out_ref,
    mask, u, vt, gv, psend, precv, ub, gu, pv,
    gs, gr, ps, pr, us, ur, gus, gur, pvs, pvr,
):
    me = lax.axis_index("prec")
    my = lax.axis_index("run")
    rows, k = u0_ref.shape
    cols = x_ref.shape[1]
    sp = rows // n // fold
    rc = rows // uchunks
    cw = cols // vchunks
    per = n // uchunks
    others = [lax.rem(me + off, n) for off in range(1, n)]
    rothers = [lax.rem(my + off, nr) for off in range(1, nr)]

    barrier = pltpu.get_barrier_semaphore()
    for d in others:
        pl.semaphore_signal(barrier, inc=1, device_id={"prec": d}, device_id_type=MESH)
    for d in rothers:
        pl.semaphore_signal(barrier, inc=1, device_id={"run": d}, device_id_type=MESH)

    def rcopy(src, dst, ss, rs, axis, d):
        return pltpu.make_async_remote_copy(
            src_ref=src, dst_ref=dst, send_sem=ss, recv_sem=rs,
            device_id={axis: d}, device_id_type=MESH,
        )

    words = w_ref.shape[1]
    wb = min(128, words)
    spread = (
        lax.broadcasted_iota(jnp.int32, (wb, 8 * wb), 0)
        == lax.broadcasted_iota(jnp.int32, (wb, 8 * wb), 1) // 8
    ).astype(f32).astype(bf16)
    for c in range(words // wb):
        for r0 in range(0, rows, 128):
            part = w_ref[r0 : r0 + 128, c * wb : (c + 1) * wb].astype(f32).astype(bf16)
            wide = mm(part, spread).astype(jnp.int32)
            lane = lax.broadcasted_iota(jnp.int32, wide.shape, 1) & 7
            bit = lax.shift_right_logical(wide, lane) & 1
            mask[r0 : r0 + 128, c * 8 * wb : (c + 1) * 8 * wb] = bit.astype(f32).astype(bf16)

    u[...] = u0_ref[...]
    eye = (
        lax.broadcasted_iota(jnp.int32, (k, k), 0) == lax.broadcasted_iota(jnp.int32, (k, k), 1)
    ).astype(f32).astype(bf16)
    for c in range(vchunks):
        vt[:, c * cw : (c + 1) * cw] = mm_nt(eye, v0_ref[c * cw : (c + 1) * cw, :]).astype(bf16)

    def share_of(x, d):
        base = d * sp * fold
        parts = [x[base + f * sp : base + (f + 1) * sp, :] for f in range(fold)]
        return parts[0] if fold == 1 else jnp.concatenate(parts, axis=1)

    start = u0_ref[...].astype(f32)
    for d in range(n):
        ub[d] = share_of(start, d).astype(bf16)

    def resid(r0, r1, c0, c1, fit):
        m = mask[r0:r1, c0:c1].astype(f32)
        return (m * (x_ref[r0:r1, c0:c1].astype(f32) - fit)).astype(bf16)

    pl.semaphore_wait(barrier, n - 1 + nr - 1)

    def iteration(it, carry):
        par = lax.rem(it, 2)
        gv[me] = pack_gram(mm_nt(vt[...], vt[...]))
        for d in others:
            rcopy(gv.at[me], gv.at[me], gs.at[d], gr.at[me], "prec", d).start()
        for c in range(uchunks):
            r0, r1 = c * rc, (c + 1) * rc
            fit = mm(u[r0:r1, :], vt[...])
            proj = mm_nt(resid(r0, r1, 0, cols, fit), vt[...])
            for i in range(per):
                psend[c * per + i] = share_of(proj, i).astype(bf16)
            for i in range(per):
                d = c * per + i

                @pl.when(me != d)
                def _():
                    rcopy(psend.at[d], precv.at[me], ps.at[d], pr.at[me], "prec", d).start()

        for d in others:
            rcopy(gv.at[me], gv.at[d], gs.at[d], gr.at[d], "prec", d).wait_recv()
        total = gv[0]
        for d in range(1, n):
            total = total + gv[d]
        inv = spd_inverse(unpack_gram(total))
        for d in others:
            rcopy(psend.at[d], precv.at[d], ps.at[d], pr.at[d], "prec", d).wait_recv()
        share = psend[me].astype(f32)
        for d in others:
            share = share + precv[d].astype(f32)
        old = ub[me].astype(f32)
        dhi, dlo = split(share - ridge_value * old)
        ihi, ilo = split(inv)
        steps = []
        for f in range(fold):
            h, l = dhi[:, f * k : (f + 1) * k], dlo[:, f * k : (f + 1) * k]
            steps.append(mm(h, ihi) + mm(h, ilo) + mm(l, ihi))
        step = steps[0] if fold == 1 else jnp.concatenate(steps, axis=1)
        ub[me] = (old + step).astype(bf16)
        for d in others:
            rcopy(ub.at[me], ub.at[me], us.at[d], ur.at[me], "prec", d).start()
        for d in others:
            rcopy(gv.at[me], gv.at[d], gs.at[d], gr.at[d], "prec", d).wait_send()
            rcopy(psend.at[d], precv.at[d], ps.at[d], pr.at[d], "prec", d).wait_send()
        for d in others:
            rcopy(ub.at[me], ub.at[d], us.at[d], ur.at[d], "prec", d).wait()
        for d in range(n):
            base = d * sp * fold
            for f in range(fold):
                u[base + f * sp : base + (f + 1) * sp, :] = ub[d][:, f * k : (f + 1) * k]

        now = u[...]
        ut = mm_nt(eye, now).astype(bf16)
        gu[par, my] = pack_gram(mm_nt(ut, ut))
        for d in rothers:
            rcopy(gu.at[par, my], gu.at[par, my], gus.at[d], gur.at[par, my], "run", d).start()
        for c in range(vchunks):
            c0, c1 = c * cw, (c + 1) * cw
            fit = mm(now, vt[:, c0:c1])
            pv[par, my, c] = mm(ut, resid(0, rows, c0, c1, fit)).astype(bf16)
            for d in rothers:
                mine = pv.at[par, my, c]
                rcopy(mine, mine, pvs.at[d, c], pvr.at[par, my, c], "run", d).start()
        for d in rothers:
            rcopy(gu.at[par, my], gu.at[par, d], gus.at[d], gur.at[par, d], "run", d).wait()
        total = gu[par, 0]
        for d in range(1, nr):
            total = total + gu[par, d]
        ihi, ilo = split(spd_inverse(unpack_gram(total)))
        lhs = jnp.concatenate([ihi, ilo, ihi], axis=1)
        for c in range(vchunks):
            c0, c1 = c * cw, (c + 1) * cw
            for d in rothers:
                rcopy(
                    pv.at[par, my, c], pv.at[par, d, c], pvs.at[d, c], pvr.at[par, d, c], "run", d
                ).wait()
            share = pv[par, 0, c].astype(f32)
            for d in range(1, nr):
                share = share + pv[par, d, c].astype(f32)
            old = vt[:, c0:c1].astype(f32)
            dhi, dlo = split(share - ridge_value * old)
            step = mm(lhs, jnp.concatenate([dhi, dhi, dlo], axis=0))
            vt[:, c0:c1] = (old + step).astype(bf16)
        return carry

    lax.fori_loop(0, ITERS, iteration, 0)

    for c in range(vchunks):
        c0, c1 = c * cw, (c + 1) * cw
        fit = mm(u[...], vt[:, c0:c1])
        m = mask[:, c0:c1].astype(f32)
        out_ref[:, c0:c1] = (m * x_ref[:, c0:c1].astype(f32) + (1.0 - m) * fit).astype(bf16)


def local(n, nr, intensity, observed, run_factors, prec_factors):
    rows, cols = intensity.shape
    k = run_factors.shape[1]
    fold = 2 if rows // n % 32 == 0 else 1
    sp = rows // n // fold
    uchunks = 4
    vchunks = max(1, min(4, cols // 128))
    cw = cols // vchunks
    dma = pltpu.SemaphoreType.DMA
    vmem = pl.BlockSpec(memory_space=pltpu.VMEM)
    return pl.pallas_call(
        functools.partial(als_kernel, n, nr, fold, uchunks, vchunks),
        out_shape=jax.ShapeDtypeStruct((rows, cols), bf16),
        in_specs=[vmem] * 4,
        out_specs=vmem,
        scratch_shapes=[
            pltpu.VMEM((rows, cols), bf16),
            pltpu.VMEM((rows, k), bf16),
            pltpu.VMEM((k, cols), bf16),
            pltpu.VMEM((n, k // 2, 2 * k), f32),
            pltpu.VMEM((n, sp, k * fold), bf16),
            pltpu.VMEM((n, sp, k * fold), bf16),
            pltpu.VMEM((n, sp, k * fold), bf16),
            pltpu.VMEM((2, nr, k // 2, 2 * k), f32),
            pltpu.VMEM((2, nr, vchunks, k, cw), bf16),
            dma((n,)), dma((n,)), dma((n,)), dma((n,)), dma((n,)), dma((n,)),
            dma((nr,)), dma((2, nr)), dma((nr, vchunks)), dma((2, nr, vchunks)),
        ],
        compiler_params=pltpu.CompilerParams(
            collective_id=0, has_side_effects=True, vmem_limit_bytes=60 << 20
        ),
    )(intensity, observed, run_factors, prec_factors)


def solution(mesh):
    n, nr = mesh.shape["prec"], mesh.shape["run"]
    return jax.shard_map(
        functools.partial(local, n, nr),
        mesh=mesh,
        in_specs=(P("run", "prec"), P("run", "prec"), P("run", None), P("prec", None)),
        out_specs=P("run", "prec"),
        check_vma=False,
    )
```

```python
import functools

import jax
import jax.numpy as jnp
from jax import lax
from jax.experimental import pallas as pl
from jax.experimental.pallas import tpu as pltpu
from jax.sharding import PartitionSpec as P

ITERS = 4
ridge_value = 16.0
f32 = jnp.float32
bf16 = jnp.bfloat16
MESH = pl.DeviceIdType.MESH
VMEM_LIMIT = 32 << 20


def mm(a, b):
    return lax.dot_general(a, b, (((1,), (0,)), ((), ())), preferred_element_type=f32)


def mm_nt(a, b):
    return lax.dot_general(a, b, (((1,), (1,)), ((), ())), preferred_element_type=f32)


def spd_inverse(a):
    size = a.shape[0]
    wide = 2 * size
    rid = lax.broadcasted_iota(jnp.int32, (size, wide), 0)
    eye = (
        lax.broadcasted_iota(jnp.int32, (size, size), 0)
        == lax.broadcasted_iota(jnp.int32, (size, size), 1)
    ).astype(f32)
    m = jnp.concatenate([a + ridge_value * eye, eye], axis=1)
    group = 4
    for k0 in range(0, size, group):
        cols = [
            jnp.broadcast_to(m[:, k0 + j : k0 + j + 1], (size, wide)) for j in range(group)
        ]
        for j in range(group):
            k = k0 + j
            inv = 1.0 / cols[j][k : k + 1, :]
            prow = m[k : k + 1, :] * inv
            m = jnp.where(rid == k, prow, m - cols[j] * prow)
            for n in range(j + 1, group):
                f = cols[j][k0 + n : k0 + n + 1, :] * inv
                cols[n] = jnp.where(rid == k, f, cols[n] - cols[j] * f)
    return m[:, size:]


def split(x):
    hi = x.astype(bf16)
    return hi, (x - hi.astype(f32)).astype(bf16)


def pack_gram(g):
    h = g.shape[0] // 2
    return jnp.concatenate([g[:h], g[h:]], axis=1)


def unpack_gram(x):
    h = x.shape[1] // 2
    return jnp.concatenate([x[:, :h], x[:, h:]], axis=0)


def als_kernel(
    n, nr, group, fold, vchunks,
    x_hbm, w_ref, ut0_ref, vt0_ref, out_ref,
    x_ref, mask, u, vt, pacc, gv1, gv2, psend, precv, ub, gu, pv,
    xs, g1s, g1r, g2s, g2r, ps, pr, us, ur, gus, gur, pvs, pvr,
):
    me = lax.axis_index("prec")
    my = lax.axis_index("run")
    k, rows = ut0_ref.shape
    cols = vt0_ref.shape[1]
    sp = rows // n // fold
    cw = cols // vchunks
    planes = n // group
    plane, seat = me // group, lax.rem(me, group)
    others = [lax.rem(me + off, n) for off in range(1, n)]
    seats = [lax.rem(seat + off, group) for off in range(1, group)]
    levels = [lax.rem(plane + off, planes) for off in range(1, planes)]
    rothers = [lax.rem(my + off, nr) for off in range(1, nr)]

    load = pltpu.make_async_copy(x_hbm, x_ref, xs)
    load.start()
    barrier = pltpu.get_barrier_semaphore()
    for d in others:
        pl.semaphore_signal(barrier, inc=1, device_id={"prec": d}, device_id_type=MESH)
    for d in rothers:
        pl.semaphore_signal(barrier, inc=1, device_id={"run": d}, device_id_type=MESH)

    def rcopy(src, dst, ss, rs, axis, d):
        return pltpu.make_async_remote_copy(
            src_ref=src, dst_ref=dst, send_sem=ss, recv_sem=rs,
            device_id={axis: d}, device_id_type=MESH,
        )

    words = w_ref.shape[1]
    wb = min(128, words)
    spread = (
        lax.broadcasted_iota(jnp.int32, (wb, 8 * wb), 0)
        == lax.broadcasted_iota(jnp.int32, (wb, 8 * wb), 1) // 8
    ).astype(f32).astype(bf16)
    for c in range(words // wb):
        for r0 in range(0, rows, 128):
            part = w_ref[r0 : r0 + 128, c * wb : (c + 1) * wb].astype(f32).astype(bf16)
            wide = mm(part, spread).astype(jnp.int32)
            lane = lax.broadcasted_iota(jnp.int32, wide.shape, 1) & 7
            bit = lax.shift_right_logical(wide, lane) & 1
            mask[r0 : r0 + 128, c * 8 * wb : (c + 1) * 8 * wb] = bit.astype(f32).astype(bf16)

    eye = (
        lax.broadcasted_iota(jnp.int32, (k, k), 0) == lax.broadcasted_iota(jnp.int32, (k, k), 1)
    ).astype(f32).astype(bf16)

    def share_of(x, d):
        base = d * sp * fold
        parts = [x[base + f * sp : base + (f + 1) * sp, :] for f in range(fold)]
        return parts[0] if fold == 1 else jnp.concatenate(parts, axis=1)

    start = jnp.transpose(ut0_ref[...].astype(f32))
    u[...] = start.astype(bf16)
    for d in range(n):
        ub[d] = share_of(start, d).astype(bf16)
    vt[...] = vt0_ref[...]

    def resid(c0, c1, fit):
        m = mask[:, c0:c1].astype(f32)
        return (m * (x_ref[:, c0:c1].astype(f32) - fit)).astype(bf16)

    def g1(d):
        return rcopy(gv1.at[seat], gv1.at[seat], g1s.at[d], g1r.at[seat], "prec", plane * group + d)

    def g1_in(d):
        return rcopy(gv1.at[seat], gv1.at[d], g1s.at[d], g1r.at[d], "prec", plane * group + d)

    def g2(d):
        return rcopy(gv2.at[plane], gv2.at[plane], g2s.at[d], g2r.at[plane], "prec", d * group + seat)

    def g2_in(d):
        return rcopy(gv2.at[plane], gv2.at[d], g2s.at[d], g2r.at[d], "prec", d * group + seat)

    def p_out(d):
        return rcopy(psend.at[d], precv.at[me], ps.at[d], pr.at[me], "prec", d)

    def p_in(d):
        return rcopy(psend.at[d], precv.at[d], ps.at[d], pr.at[d], "prec", d)

    def launch_u(update):
        gram = None
        for c in range(vchunks):
            c0, c1 = c * cw, (c + 1) * cw
            if update is not None:
                update(c)
            v = vt[:, c0:c1]
            gram = mm_nt(v, v) if gram is None else gram + mm_nt(v, v)
            if c == vchunks - 1:
                gv1[seat] = pack_gram(gram)
                for d in seats:
                    g1(d).start()
            proj = mm_nt(resid(c0, c1, mm(u[...], v)), v)
            pacc[...] = proj if c == 0 else pacc[...] + proj
        for d in range(n):
            psend[d] = share_of(pacc, d).astype(bf16)
        for d in others:
            p_out(d).start()

    def finish_u():
        for d in seats:
            g1_in(d).wait_recv()
        total = gv1[0]
        for d in range(1, group):
            total = total + gv1[d]
        gv2[plane] = total
        for d in levels:
            g2(d).start()
        for d in levels:
            g2_in(d).wait_recv()
        total = gv2[0]
        for d in range(1, planes):
            total = total + gv2[d]
        ihi, ilo = split(spd_inverse(unpack_gram(total)))
        for d in others:
            p_in(d).wait_recv()
        share = psend[me].astype(f32)
        for d in others:
            share = share + precv[d].astype(f32)
        old = ub[me].astype(f32)
        dhi, dlo = split(share - ridge_value * old)
        steps = []
        for f in range(fold):
            h, l = dhi[:, f * k : (f + 1) * k], dlo[:, f * k : (f + 1) * k]
            steps.append(mm(h, ihi) + mm(h, ilo) + mm(l, ihi))
        step = steps[0] if fold == 1 else jnp.concatenate(steps, axis=1)
        ub[me] = (old + step).astype(bf16)
        for d in others:
            rcopy(ub.at[me], ub.at[me], us.at[d], ur.at[me], "prec", d).start()
        for d in seats:
            g1_in(d).wait_send()
        for d in levels:
            g2_in(d).wait_send()
        for d in others:
            p_in(d).wait_send()
        for d in others:
            rcopy(ub.at[me], ub.at[d], us.at[d], ur.at[d], "prec", d).wait()
        for d in range(n):
            base = d * sp * fold
            for f in range(fold):
                u[base + f * sp : base + (f + 1) * sp, :] = ub[d][:, f * k : (f + 1) * k]

    def launch_v(par):
        now = u[...]
        ut = mm_nt(eye, now).astype(bf16)
        gu[par, my] = pack_gram(mm_nt(ut, ut))
        for d in rothers:
            rcopy(gu.at[par, my], gu.at[par, my], gus.at[d], gur.at[par, my], "run", d).start()
        for c in range(vchunks):
            c0, c1 = c * cw, (c + 1) * cw
            fit = mm(now, vt[:, c0:c1])
            pv[par, my, c] = mm(ut, resid(c0, c1, fit)).astype(bf16)
            for d in rothers:
                mine = pv.at[par, my, c]
                rcopy(mine, mine, pvs.at[d, c], pvr.at[par, my, c], "run", d).start()
        for d in rothers:
            rcopy(gu.at[par, my], gu.at[par, d], gus.at[d], gur.at[par, d], "run", d).wait()
        total = gu[par, 0]
        for d in range(1, nr):
            total = total + gu[par, d]
        ihi, ilo = split(spd_inverse(unpack_gram(total)))
        lhs = jnp.concatenate([ihi, ilo, ihi], axis=1)

        def update(c):
            c0, c1 = c * cw, (c + 1) * cw
            for d in rothers:
                rcopy(
                    pv.at[par, my, c], pv.at[par, d, c], pvs.at[d, c], pvr.at[par, d, c], "run", d
                ).wait()
            share = pv[par, 0, c].astype(f32)
            for d in range(1, nr):
                share = share + pv[par, d, c].astype(f32)
            old = vt[:, c0:c1].astype(f32)
            dhi, dlo = split(share - ridge_value * old)
            step = mm(lhs, jnp.concatenate([dhi, dhi, dlo], axis=0))
            vt[:, c0:c1] = (old + step).astype(bf16)

        return update

    load.wait()
    pl.semaphore_wait(barrier, n - 1 + nr - 1)
    launch_u(None)

    def iteration(it, carry):
        finish_u()
        launch_u(launch_v(lax.rem(it, 2)))
        return carry

    lax.fori_loop(0, ITERS - 1, iteration, 0)
    finish_u()
    update = launch_v((ITERS - 1) % 2)
    for c in range(vchunks):
        c0, c1 = c * cw, (c + 1) * cw
        update(c)
        fit = mm(u[...], vt[:, c0:c1])
        m = mask[:, c0:c1].astype(f32)
        out_ref[:, c0:c1] = (m * x_ref[:, c0:c1].astype(f32) + (1.0 - m) * fit).astype(bf16)


def local(n, nr, intensity, observed, run_factors, prec_factors):
    rows, cols = intensity.shape
    k = run_factors.shape[1]
    fold = 2 if rows // n % 32 == 0 else 1
    sp = rows // n // fold
    group = 1
    while group * group * 4 <= n:
        group *= 2
    vchunks = max(1, min(4, cols // 128))
    cw = cols // vchunks
    dma = pltpu.SemaphoreType.DMA
    vmem = pl.BlockSpec(memory_space=pltpu.VMEM)
    return pl.pallas_call(
        functools.partial(als_kernel, n, nr, group, fold, vchunks),
        out_shape=jax.ShapeDtypeStruct((rows, cols), bf16),
        in_specs=[pl.BlockSpec(memory_space=pl.ANY)] + [vmem] * 3,
        out_specs=vmem,
        scratch_shapes=[
            pltpu.VMEM((rows, cols), bf16),
            pltpu.VMEM((rows, cols), bf16),
            pltpu.VMEM((rows, k), bf16),
            pltpu.VMEM((k, cols), bf16),
            pltpu.VMEM((rows, k), f32),
            pltpu.VMEM((group, k // 2, 2 * k), f32),
            pltpu.VMEM((n // group, k // 2, 2 * k), f32),
            pltpu.VMEM((n, sp, k * fold), bf16),
            pltpu.VMEM((n, sp, k * fold), bf16),
            pltpu.VMEM((n, sp, k * fold), bf16),
            pltpu.VMEM((2, nr, k // 2, 2 * k), f32),
            pltpu.VMEM((2, nr, vchunks, k, cw), bf16),
            dma(()),
            dma((group,)), dma((group,)), dma((n // group,)), dma((n // group,)),
            dma((n,)), dma((n,)), dma((n,)), dma((n,)),
            dma((nr,)), dma((2, nr)), dma((nr, vchunks)), dma((2, nr, vchunks)),
        ],
        compiler_params=pltpu.CompilerParams(
            collective_id=0, has_side_effects=True, vmem_limit_bytes=VMEM_LIMIT
        ),
    )(intensity, observed, run_factors.T, prec_factors.T)


def solution(mesh):
    n, nr = mesh.shape["prec"], mesh.shape["run"]
    return jax.shard_map(
        functools.partial(local, n, nr),
        mesh=mesh,
        in_specs=(P("run", "prec"), P("run", "prec"), P("run", None), P("prec", None)),
        out_specs=P("run", "prec"),
        check_vma=False,
    )
```
